32 devices in a mesh: tm: 8 (over z, x), rows: 4 (over y, core).
Axes of the slice: x: 2, y: 2, z: 4, core: 2. Of those that a mesh axis runs over, the one named last changes fastest.
Arguments:
- drift_blocks: bfloat16 [128, 4, 128, 128], P('rows'), may hold values from -0.1875 to 0.1875
- drift_cols: int32 [128, 4], P('rows'), may hold values from 0 to 127
- control_blocks: bfloat16 [4, 128, 128, 128], P(None, 'rows'), may hold values from -0.1875 to 0.1875
- control_cols: int32 [4, 128], P(None, 'rows'), may hold values from 0 to 127
- controls: float32 [4, 40, 8], P(None, 'tm'), may hold values from -4 to 4
- shooting_states: bfloat16 [8, 8, 16384], P('tm', None, 'rows'), may hold values from -6 to 6
- targets: bfloat16 [40, 8, 16384], P('tm', None, 'rows'), may hold values from -6 to 6
Outputs:
- grad_shooting: float32 [8, 8, 16384], P('tm', None, 'rows')
- grad_controls: float32 [4, 40, 8], P(None, 'tm')
- grad_drift: float32 [128, 65536], P('rows', 'tm')
- grad_control_ops: float32 [4, 128, 16384], P(None, 'rows', 'tm')
The draws below stay inside these ranges and needn't reach their ends.
Inputs may be any that keep to these rules, and one draw needn't show every extreme that they name: `drift_cols`: block column index of each stored drift block; several stored blocks may share a column. `control_cols`: block column index of each stored control block.
All inputs are finite; a program needn't handle non-finite values.
Results may differ from the reference program's by a relative error of at most 0.02.
Values may be sent and summed in bfloat16 or wider, within the bound.
A program may use at most 128 MiB of HBM per device.

```python
import jax
import jax.numpy as jnp
from jax import lax

NL = 16384
BS = 128
NB = 128
K = 4
NU = 4
S = 8
L = 5
NC = 8
H = 40


def set_ends(drawn, key, least, largest):
    shape = drawn.shape
    spot = [jax.random.randint(jax.random.fold_in(key, axis), (), 0, shape[axis]) for axis in range(len(shape))]
    drawn = drawn.at[tuple(spot)].set(least)
    longest = shape.index(max(shape))
    spot[longest] = (spot[longest] + 1) % shape[longest]
    return drawn.at[tuple(spot)].set(largest)


def steps_of(stream_key, shape, split, low, top_value):
    level = 1.0
    for dim, shards_of in split:
        steps = jax.random.uniform(jax.random.fold_in(jax.random.fold_in(stream_key, 6), dim), (shards_of,), jnp.float32, low / len(split), top_value / len(split))
        level = level * jnp.repeat(jnp.exp(steps), shape[dim] // shards_of).reshape((-1,) + (1,) * (len(shape) - 1 - dim))
    return level


def gaussian(own_key, shape, deviation, bound, cuts=(), held_as=jnp.bfloat16):
    drawn = deviation * jax.random.normal(own_key, shape, jnp.float32)
    if cuts:
        drawn = drawn * steps_of(own_key, shape, cuts, -0.22, 0.18)
    return jnp.clip(drawn, -bound, bound).astype(held_as)


def setup_inputs(seed: int = 0) -> dict:
    key_of = jax.random.split(jax.random.key(seed), 8)
    return {
        "drift_blocks": gaussian(key_of[0], (NB, K, BS, BS), (2 * K * BS) ** -0.5, 0.1875, ((0, 4),)),
        "drift_cols": set_ends(jax.random.randint(key_of[1], (NB, K), 0, NB), jax.random.fold_in(key_of[1], 1), 0, NB - 1).astype(jnp.int32),
        "control_blocks": gaussian(key_of[2], (NU, NB, BS, BS), (2 * BS * NU) ** -0.5, 0.1875, ((1, 4),)),
        "control_cols": set_ends(jax.random.randint(key_of[3], (NU, NB), 0, NB), jax.random.fold_in(key_of[3], 1), 0, NB - 1).astype(jnp.int32),
        "controls": gaussian(key_of[4], (NU, H, S), 1.0, 4.0, ((1, 8),), jnp.float32),
        "shooting_states": gaussian(key_of[5], (NC, S, NL), 1.0, 6.0, ((0, 8), (2, 4))),
        "targets": gaussian(key_of[6], (H, S, NL), 1.0, 6.0, ((0, 8), (2, 4))),
    }


defect_weight = 2.0


def to_half(value):
    return lax.optimization_barrier(value.astype(jnp.bfloat16))


def step_terms(state_panel, drift_blocks, drift_cols, control_blocks, control_cols):
    blocks = state_panel.reshape(S, NB, BS).astype(jnp.float32)
    picked = blocks[:, drift_cols]
    drift_out = jnp.einsum('snki,nkoi->sno', picked, drift_blocks.astype(jnp.float32))
    control_picked = blocks[:, control_cols]
    control_out = jnp.einsum('sjni,jnoi->sjno', control_picked, control_blocks.astype(jnp.float32))
    return picked, drift_out, control_picked, control_out


def forward_group(first_panel, group_inputs, operators):
    panels = [first_panel]
    state_panel = first_panel
    for position in range(L):
        picked, drift_out, control_picked, control_out = step_terms(state_panel, *operators)
        weights = group_inputs[:, position].T[:, :, None, None]
        mixed = drift_out + jnp.sum(weights * control_out, axis=1)
        state_panel = to_half(mixed.reshape(S, NL))
        panels.append(state_panel)
    return panels


def reference(drift_blocks, drift_cols, control_blocks, control_cols, controls, shooting_states, targets):
    operators = (drift_blocks, drift_cols, control_blocks, control_cols)
    indices = jnp.arange(NC, dtype=jnp.int32)

    def group_controls(group_index):
        return lax.dynamic_slice_in_dim(controls, (group_index * L).astype(jnp.int32), L, 1)

    def end_of(group_index):
        return forward_group(shooting_states[group_index], group_controls(group_index), operators)[-1]

    group_ends = lax.map(end_of, indices)

    def backward(carry, group_index):
        drift_sum, control_sum = carry
        group_inputs = group_controls(group_index)
        group_targets = lax.dynamic_slice_in_dim(targets, (group_index * L).astype(jnp.int32), L, 0)
        panels = forward_group(shooting_states[group_index], group_inputs, operators)
        next_start = shooting_states[jnp.minimum(group_index + 1, NC - 1)].astype(jnp.float32)
        prev_end = group_ends[jnp.maximum(group_index - 1, 0)].astype(jnp.float32)
        group_end = panels[-1].astype(jnp.float32)
        defect = jnp.where(group_index < NC - 1, next_start - group_end, 0.0)
        prev_defect = jnp.where(group_index > 0, shooting_states[group_index].astype(jnp.float32) - prev_end, 0.0)
        adjoint = group_end - group_targets[L - 1].astype(jnp.float32) - defect_weight * defect
        input_grads = [None] * L
        for position in reversed(range(L)):
            adjoint_half = to_half(adjoint).astype(jnp.float32)
            picked, drift_out, control_picked, control_out = step_terms(panels[position], *operators)
            mu_blocks = adjoint_half.reshape(S, NB, BS)
            weights = group_inputs[:, position].T[:, :, None, None]
            input_grads[position] = jnp.sum(mu_blocks[:, None] * control_out, axis=(2, 3)).T
            drift_sum = drift_sum + jnp.einsum('sno,snki->nkoi', mu_blocks, picked)
            weighted = to_half(mu_blocks[:, None] * weights).astype(jnp.float32)
            control_sum = control_sum + jnp.einsum('sjno,sjni->jnoi', weighted, control_picked)
            drift_back = jnp.einsum('sno,nkoi->snki', mu_blocks, drift_blocks.astype(jnp.float32))
            control_back = jnp.einsum('sno,jnoi->sjni', mu_blocks, control_blocks.astype(jnp.float32)) * weights
            spread = jnp.zeros((S, NB, BS), jnp.float32)
            spread = spread.at[:, drift_cols].add(drift_back).at[:, control_cols].add(control_back)
            adjoint = spread.reshape(S, NL)
            if position > 0:
                adjoint = adjoint + panels[position].astype(jnp.float32) - group_targets[position - 1].astype(jnp.float32)
        grad_shoot = adjoint + defect_weight * prev_defect
        return (drift_sum, control_sum), (grad_shoot, jnp.stack(input_grads, 1))

    start = (jnp.zeros((NB, K, BS, BS), jnp.float32), jnp.zeros((NU, NB, BS, BS), jnp.float32))
    (drift_sum, control_sum), (grad_shooting, input_grads) = lax.scan(backward, start, indices)
    grad_controls = jnp.transpose(input_grads, (1, 0, 2, 3)).reshape(NU, H, S) * (NL ** -0.5)
    grad_scale = (S * H) ** -0.5
    grad_drift = drift_sum.reshape(NB, K * BS * BS) * grad_scale
    grad_control_ops = control_sum.reshape(NU, NB, BS * BS) * grad_scale
    return grad_shooting, grad_controls, grad_drift, grad_control_ops
```

```python
import jax
import jax.numpy as jnp
from jax import lax
from jax.sharding import PartitionSpec as P

defect_weight = 2.0


def passed_along(value, axis, by):
    count = lax.axis_size(axis)
    pairs = [(i, i + by) for i in range(count) if 0 <= i + by < count]
    return lax.ppermute(value, axis, pairs)


def step_terms(gathered, block_width, drift_blocks, drift_cols, control_blocks, control_cols):
    blocks = gathered.reshape(gathered.shape[0], -1, block_width)
    picked = blocks[:, drift_cols]
    drift_out = jnp.einsum(
        "snki,nkoi->sno", picked, drift_blocks, preferred_element_type=jnp.float32
    )
    control_picked = blocks[:, control_cols]
    control_out = jnp.einsum(
        "sjni,jnoi->sjno", control_picked, control_blocks, preferred_element_type=jnp.float32
    )
    return (picked, drift_out, control_picked, control_out)


def shards(
    drift_blocks, drift_cols, control_blocks, control_cols, controls, shooting_states, targets
):
    block_width = drift_blocks.shape[-1]
    scenarios = shooting_states.shape[1]
    local_rows = shooting_states.shape[2]
    horizon_steps = targets.shape[0]
    group_count = lax.axis_size("tm")
    group_index = lax.axis_index("tm")
    total_blocks = drift_blocks.shape[0] * lax.axis_size("rows")
    lifted_total = local_rows * lax.axis_size("rows")
    operators = (drift_blocks, drift_cols, control_blocks, control_cols)
    row_count = lax.axis_size("rows")
    targets_of = jnp.concatenate([drift_cols.reshape(-1), control_cols.reshape(-1)])
    hits = (targets_of[:, None] == jnp.arange(total_blocks)[None]).astype(jnp.bfloat16)
    first_panel = shooting_states[0]
    panels = [first_panel]
    stored = []
    full_states = []
    state_panel = first_panel
    for position in range(horizon_steps):
        gathered = lax.all_gather(state_panel, "rows", axis=1, tiled=True)
        full_states.append(gathered)
        step_parts = step_terms(gathered, block_width, *operators)
        stored.append(step_parts)
        weights = controls[:, position].T[:, :, None, None]
        mixed = step_parts[1] + jnp.sum(weights * step_parts[3], axis=1)
        state_panel = mixed.reshape(scenarios, local_rows).astype(jnp.bfloat16)
        panels.append(state_panel)
    group_end = panels[-1]
    next_start = passed_along(first_panel, "tm", -1)
    prev_end = passed_along(group_end, "tm", 1)
    end_wide = group_end.astype(jnp.float32)
    defect = jnp.where(
        group_index < group_count - 1, next_start.astype(jnp.float32) - end_wide, 0.0
    )
    prev_defect = jnp.where(
        group_index > 0, first_panel.astype(jnp.float32) - prev_end.astype(jnp.float32), 0.0
    )
    adjoint = end_wide - targets[horizon_steps - 1].astype(jnp.float32) - defect_weight * defect
    input_grads = [None] * horizon_steps
    mu_list = []
    picked_list = []
    weighted_list = []
    control_picked_list = []
    for position in reversed(range(horizon_steps)):
        adjoint_half = adjoint.astype(jnp.bfloat16)
        picked, drift_out, control_picked, control_out = stored[position]
        mu_blocks = adjoint_half.reshape(scenarios, -1, block_width)
        mu_wide = mu_blocks.astype(jnp.float32)
        weights = controls[:, position].T[:, :, None, None]
        input_grads[position] = jnp.sum(mu_wide[:, None] * control_out, axis=(2, 3)).T
        weighted = (mu_wide[:, None] * weights).astype(jnp.bfloat16)
        mu_list.append(mu_blocks)
        picked_list.append(picked)
        weighted_list.append(weighted)
        control_picked_list.append(control_picked)
        drift_back = jnp.einsum(
            "sno,nkoi->snki", mu_blocks, drift_blocks, preferred_element_type=jnp.float32
        )
        control_back = (
            jnp.einsum(
                "sno,jnoi->sjni", mu_blocks, control_blocks, preferred_element_type=jnp.float32
            )
            * weights
        )
        terms = jnp.concatenate(
            [
                drift_back.reshape(scenarios, -1, block_width),
                control_back.reshape(scenarios, -1, block_width),
            ],
            1,
        ).astype(jnp.bfloat16)
        spread = jnp.einsum("gc,sgi->csi", hits, terms, preferred_element_type=jnp.float32)
        spread = spread.astype(jnp.bfloat16).reshape(row_count, -1, scenarios, block_width)
        shares = lax.all_to_all(spread, "rows", 0, 0)
        total = jnp.sum(shares.astype(jnp.float32), 0)
        adjoint = jnp.swapaxes(total, 0, 1).reshape(scenarios, local_rows)
        if position > 0:
            adjoint = (
                adjoint
                + panels[position].astype(jnp.float32)
                - targets[position - 1].astype(jnp.float32)
            )
    grad_shooting = (adjoint + defect_weight * prev_defect)[None]
    grad_controls = lax.psum(jnp.stack(input_grads, 1), "rows") * lifted_total ** (-0.5)
    grad_scale = (scenarios * horizon_steps * group_count) ** (-0.5)
    slots, controls_count = drift_cols.shape[1], control_cols.shape[0]
    rows_here = drift_blocks.shape[0]
    if group_count // 2 == slots:
        pair_groups = [[i for i in range(group_count) if i % 2 == b] for b in range(2)]
        pair = group_index // 2
        half = group_index % 2

        def along(value):
            return lax.all_gather(value, "tm", axis_index_groups=pair_groups)

        states = along(jnp.stack(full_states)).reshape(-1, total_blocks, block_width)
        inputs = along(controls).transpose(0, 2, 3, 1).reshape(-1, controls_count)
        mus = along(jnp.stack(mu_list[::-1])).reshape(-1, rows_here, block_width)
        col = lax.dynamic_index_in_dim(drift_cols, pair, 1, keepdims=False)
        drift_sum = jnp.einsum(
            "tno,tni->noi", mus, states[:, col], preferred_element_type=jnp.float32
        )
        span = block_width // slots
        mus_cut = lax.dynamic_slice_in_dim(mus, pair * span, span, 2)
        weighted = (mus_cut.astype(jnp.float32)[:, None] * inputs[:, :, None, None]).astype(
            jnp.bfloat16
        )
        control_sum = jnp.einsum(
            "tjno,tjni->jnoi", weighted, states[:, control_cols], preferred_element_type=jnp.float32
        )
        drift_two = drift_sum.reshape(rows_here, 2, -1)
        control_two = control_sum.reshape(controls_count, rows_here, 2, -1)
        swap = [(i, i ^ 1) for i in range(group_count)]

        def merged(two, axis):
            mine = lax.dynamic_index_in_dim(two, half, axis, keepdims=False)
            other = lax.dynamic_index_in_dim(two, 1 - half, axis, keepdims=False)
            got = lax.ppermute(other.astype(jnp.bfloat16), "tm", swap)
            return (mine + got.astype(jnp.float32)) * grad_scale

        return (grad_shooting, grad_controls, merged(drift_two, 1), merged(control_two, 2))
    all_mu = jnp.concatenate(mu_list, 0)
    all_picked = jnp.concatenate(picked_list, 0)
    drift_sum = jnp.einsum("sno,snki->nkoi", all_mu, all_picked, preferred_element_type=jnp.float32)
    all_weighted = jnp.concatenate(weighted_list, 0)
    all_control_picked = jnp.concatenate(control_picked_list, 0)
    control_sum = jnp.einsum(
        "sjno,sjni->jnoi", all_weighted, all_control_picked, preferred_element_type=jnp.float32
    )
    drift_flat = drift_sum.reshape(drift_sum.shape[0], -1)
    grad_drift = lax.psum_scatter(drift_flat, "tm", scatter_dimension=1, tiled=True) * grad_scale
    control_flat = control_sum.reshape(control_sum.shape[0], control_sum.shape[1], -1)
    grad_control_ops = (
        lax.psum_scatter(control_flat, "tm", scatter_dimension=2, tiled=True) * grad_scale
    )
    return (grad_shooting, grad_controls, grad_drift, grad_control_ops)


def solution(mesh):
    return jax.shard_map(
        shards,
        mesh=mesh,
        in_specs=(
            P("rows", None, None, None),
            P("rows", None),
            P(None, "rows", None, None),
            P(None, "rows"),
            P(None, "tm", None),
            P("tm", None, "rows"),
            P("tm", None, "rows"),
        ),
        out_specs=(
            P("tm", None, "rows"),
            P(None, "tm", None),
            P("rows", "tm"),
            P(None, "rows", "tm"),
        ),
        check_vma=False,
    )
```

```python
import jax
import jax.numpy as jnp
from jax import lax
from jax.experimental import pallas as pl
from jax.experimental.pallas import tpu as pltpu
from jax.sharding import PartitionSpec as P

defect_weight = 2.0


def passed_along(value, axis, by):
    count = lax.axis_size(axis)
    pairs = [(i, i + by) for i in range(count) if 0 <= i + by < count]
    return lax.ppermute(value, axis, pairs)


def step_terms(gathered, block_width, drift_blocks, drift_cols, control_blocks, control_cols):
    blocks = gathered.reshape(gathered.shape[0], -1, block_width)
    picked = blocks[:, drift_cols]
    drift_out = jnp.einsum(
        "snki,nkoi->sno", picked, drift_blocks, preferred_element_type=jnp.float32
    )
    control_picked = blocks[:, control_cols]
    control_out = jnp.einsum(
        "sjni,jnoi->sjno", control_picked, control_blocks, preferred_element_type=jnp.float32
    )
    return (picked, drift_out, control_picked, control_out)


def general(
    drift_blocks, drift_cols, control_blocks, control_cols, controls, shooting_states, targets
):
    block_width = drift_blocks.shape[-1]
    scenarios = shooting_states.shape[1]
    local_rows = shooting_states.shape[2]
    horizon_steps = targets.shape[0]
    group_count = lax.axis_size("tm")
    group_index = lax.axis_index("tm")
    total_blocks = drift_blocks.shape[0] * lax.axis_size("rows")
    lifted_total = local_rows * lax.axis_size("rows")
    operators = (drift_blocks, drift_cols, control_blocks, control_cols)
    row_count = lax.axis_size("rows")
    targets_of = jnp.concatenate([drift_cols.reshape(-1), control_cols.reshape(-1)])
    hits = (targets_of[:, None] == jnp.arange(total_blocks)[None]).astype(jnp.bfloat16)
    first_panel = shooting_states[0]
    panels = [first_panel]
    stored = []
    state_panel = first_panel
    for position in range(horizon_steps):
        gathered = lax.all_gather(state_panel, "rows", axis=1, tiled=True)
        step_parts = step_terms(gathered, block_width, *operators)
        stored.append(step_parts)
        weights = controls[:, position].T[:, :, None, None]
        mixed = step_parts[1] + jnp.sum(weights * step_parts[3], axis=1)
        state_panel = mixed.reshape(scenarios, local_rows).astype(jnp.bfloat16)
        panels.append(state_panel)
    group_end = panels[-1]
    next_start = passed_along(first_panel, "tm", -1)
    prev_end = passed_along(group_end, "tm", 1)
    end_wide = group_end.astype(jnp.float32)
    defect = jnp.where(
        group_index < group_count - 1, next_start.astype(jnp.float32) - end_wide, 0.0
    )
    prev_defect = jnp.where(
        group_index > 0, first_panel.astype(jnp.float32) - prev_end.astype(jnp.float32), 0.0
    )
    adjoint = end_wide - targets[horizon_steps - 1].astype(jnp.float32) - defect_weight * defect
    input_grads = [None] * horizon_steps
    mu_list = []
    picked_list = []
    weighted_list = []
    control_picked_list = []
    for position in reversed(range(horizon_steps)):
        adjoint_half = adjoint.astype(jnp.bfloat16)
        picked, drift_out, control_picked, control_out = stored[position]
        mu_blocks = adjoint_half.reshape(scenarios, -1, block_width)
        mu_wide = mu_blocks.astype(jnp.float32)
        weights = controls[:, position].T[:, :, None, None]
        input_grads[position] = jnp.sum(mu_wide[:, None] * control_out, axis=(2, 3)).T
        weighted = (mu_wide[:, None] * weights).astype(jnp.bfloat16)
        mu_list.append(mu_blocks)
        picked_list.append(picked)
        weighted_list.append(weighted)
        control_picked_list.append(control_picked)
        drift_back = jnp.einsum(
            "sno,nkoi->snki", mu_blocks, drift_blocks, preferred_element_type=jnp.float32
        )
        control_back = (
            jnp.einsum(
                "sno,jnoi->sjni", mu_blocks, control_blocks, preferred_element_type=jnp.float32
            )
            * weights
        )
        terms = jnp.concatenate(
            [
                drift_back.reshape(scenarios, -1, block_width),
                control_back.reshape(scenarios, -1, block_width),
            ],
            1,
        ).astype(jnp.bfloat16)
        spread = jnp.einsum("gc,sgi->csi", hits, terms, preferred_element_type=jnp.float32)
        spread = spread.astype(jnp.bfloat16).reshape(row_count, -1, scenarios, block_width)
        shares = lax.all_to_all(spread, "rows", 0, 0)
        total = jnp.sum(shares.astype(jnp.float32), 0)
        adjoint = jnp.swapaxes(total, 0, 1).reshape(scenarios, local_rows)
        if position > 0:
            adjoint = (
                adjoint
                + panels[position].astype(jnp.float32)
                - targets[position - 1].astype(jnp.float32)
            )
    grad_shooting = (adjoint + defect_weight * prev_defect)[None]
    grad_controls = lax.psum(jnp.stack(input_grads, 1), "rows") * lifted_total ** (-0.5)
    grad_scale = (scenarios * horizon_steps * group_count) ** (-0.5)
    all_mu = jnp.concatenate(mu_list, 0)
    all_picked = jnp.concatenate(picked_list, 0)
    drift_sum = jnp.einsum("sno,snki->nkoi", all_mu, all_picked, preferred_element_type=jnp.float32)
    all_weighted = jnp.concatenate(weighted_list, 0)
    all_control_picked = jnp.concatenate(control_picked_list, 0)
    control_sum = jnp.einsum(
        "sjno,sjni->jnoi", all_weighted, all_control_picked, preferred_element_type=jnp.float32
    )
    drift_flat = drift_sum.reshape(drift_sum.shape[0], -1)
    grad_drift = lax.psum_scatter(drift_flat, "tm", scatter_dimension=1, tiled=True) * grad_scale
    control_flat = control_sum.reshape(control_sum.shape[0], control_sum.shape[1], -1)
    grad_control_ops = (
        lax.psum_scatter(control_flat, "tm", scatter_dimension=2, tiled=True) * grad_scale
    )
    return (grad_shooting, grad_controls, grad_drift, grad_control_ops)


MESH = pl.DeviceIdType.MESH
F32, BF16 = jnp.float32, jnp.bfloat16


def sweep_kernel(
    dcol, ccol, drift, control, wts, start, nxt, tgt, hits,
    zall_out, mu_out, lam, last, ig,
    z0, z1, z2, z3, z4, zfar, muall, bz, terms, spread, outbox, inbox,
    ag_s, ag_r, zl_s, zl_r, fw_s, fw_r, mu_s, mu_r, rs_s, rs_r, loc,
):
    zs = (z0, z1, z2, z3, z4)
    steps, _, blocks, scen, width = zfar.shape
    rows = start.shape[0]
    slots, nu = drift.shape[1], control.shape[0]
    count = rows * (slots + nu)
    tm, r = lax.axis_index("tm"), lax.axis_index("rows")
    q, x = tm // 2, tm % 2
    peers = range(1, 4)

    def row_peer(d):
        return {"tm": tm, "rows": r ^ d}

    def line_peer(e):
        return {"tm": 2 * (q ^ e) + x, "rows": r}

    barrier = pltpu.get_barrier_semaphore()
    for d in peers:
        pl.semaphore_signal(barrier, inc=1, device_id=row_peer(d), device_id_type=MESH)
        pl.semaphore_signal(barrier, inc=1, device_id=line_peer(d), device_id_type=MESH)
    pl.semaphore_wait(barrier, 6)
    pending = []

    def send(src, dst, s, t, to):
        copy = pltpu.make_async_remote_copy(
            src_ref=src, dst_ref=dst, send_sem=s, recv_sem=t, device_id=to, device_id_type=MESH
        )
        copy.start()
        pending.append(copy)
        return copy

    def panel(k, row):
        return zs[k].at[pl.ds(row * rows, rows)]

    def far(k, e, row):
        return zfar.at[k, e - 1, pl.ds(row * rows, rows)]

    def gather_start(k):
        return [
            send(panel(k, r), panel(k, r), ag_s.at[k, d - 1], ag_r.at[k, d - 1], row_peer(d))
            for d in peers
        ]

    def line_start(k):
        return [
            send(
                panel(k, r ^ (2 * h)), far(k, e, r ^ (2 * h)),
                zl_s.at[k, e - 1, h], zl_r.at[k, e - 1, h], line_peer(e),
            )
            for e in peers
            for h in range(2)
        ]

    def landed_line(k, e, h):
        there = far(k, e, r ^ (2 * h))
        return pltpu.make_async_remote_copy(
            src_ref=there, dst_ref=there, send_sem=zl_s.at[k, e - 1, h],
            recv_sem=zl_r.at[k, e - 1, h], device_id=line_peer(e), device_id_type=MESH,
        )

    def pass_on(k):
        for e in peers:
            for h in range(2):
                landed_line(k, e, h).wait_recv()
                there = far(k, e, r ^ (2 * h))
                send(there, there, fw_s.at[k, e - 1, h], fw_r.at[k, e - 1, h], row_peer(1))

    zs[0][pl.ds(r * rows, rows)] = start[...]
    for k in range(steps):
        for copy in gather_start(k):
            copy.wait_recv()
        line_start(k)

        def forward(i, carry):
            acc = jnp.zeros((scen, width), F32)
            for m in range(slots):
                acc += lax.dot_general(
                    zs[k][dcol[i, m]], drift[i, m], (((1,), (1,)), ((), ())),
                    preferred_element_type=F32,
                )
            for j in range(nu):
                part = lax.dot_general(
                    zs[k][ccol[j, i]], control[j, i], (((1,), (1,)), ((), ())),
                    preferred_element_type=F32,
                )
                bz[k, j, i] = part
                acc += wts[k, j] * part
            if k + 1 < steps:
                zs[k + 1][r * rows + i] = acc.astype(BF16)
            else:
                last[i] = acc.astype(BF16)
            return carry

        lax.fori_loop(0, rows, forward, 0, unroll=4)
    ends = last[...].astype(F32)
    factor = jnp.where(tm < lax.axis_size("tm") - 1, defect_weight, 0.0)
    lam[...] = ends - tgt[steps - 1].astype(F32) - factor * (nxt[...].astype(F32) - ends)
    for k in reversed(range(steps)):
        muall[k, q] = lam[...].astype(BF16)
        for e in peers:
            send(muall.at[k, q], muall.at[k, q], mu_s.at[k, e - 1], mu_r.at[k, e - 1], line_peer(e))

        def backward(i, carry):
            mu = muall[k, q, i]
            wide = mu.astype(F32)
            for m in range(slots):
                terms[pl.ds(i * slots + m, scen, stride=count), :] = jnp.dot(
                    mu, drift[i, m], preferred_element_type=F32
                )
            sums = []
            for j in range(nu):
                sums.append(carry[j] + wide * bz[k, j, i])
                terms[pl.ds(rows * slots + i * nu + j, scen, stride=count), :] = wts[k, j] * jnp.dot(
                    mu, control[j, i], preferred_element_type=F32
                )
            return tuple(sums)

        zero = jnp.zeros((scen, width), F32)
        sums = lax.fori_loop(0, rows, backward, (zero,) * nu, unroll=4)
        for j in range(nu):
            ig[k, j] = sums[j]
        for s in range(scen):
            spread[pl.ds(s, blocks, stride=scen), :] = jnp.dot(
                hits[...], terms[pl.ds(s * count, count), :].astype(BF16),
                preferred_element_type=F32,
            )

        def share(row):
            at = pl.multiple_of(row * (rows * scen), rows * scen)
            return spread[pl.ds(at, rows * scen), :].reshape(rows, scen, width)

        arriving = []
        for d in (2, 3, 1):
            outbox[k, d - 1] = share(r ^ d).astype(BF16)
            arriving.append(
                send(outbox.at[k, d - 1], inbox.at[k, d - 1], rs_s.at[k, d - 1], rs_r.at[k, d - 1], row_peer(d))
            )
        pass_on(steps - 1 - k)
        for copy in arriving:
            copy.wait_recv()
        total = share(r)
        for d in peers:
            total += inbox[k, d - 1].astype(F32)
        if k > 0:
            total += zs[k][pl.ds(r * rows, rows)].astype(F32) - tgt[k - 1].astype(F32)
        lam[...] = total
    for k in range(steps):
        for e in peers:
            theirs = muall.at[k, q ^ e]
            pltpu.make_async_remote_copy(
                src_ref=theirs, dst_ref=theirs, send_sem=mu_s.at[k, e - 1],
                recv_sem=mu_r.at[k, e - 1], device_id=line_peer(e), device_id_type=MESH,
            ).wait_recv()
            for h in range(2):
                there = far(k, e, r ^ 1 ^ (2 * h))
                pltpu.make_async_remote_copy(
                    src_ref=there, dst_ref=there, send_sem=fw_s.at[k, e - 1, h],
                    recv_sem=fw_r.at[k, e - 1, h], device_id=row_peer(1), device_id_type=MESH,
                ).wait_recv()
    local = [pltpu.make_async_copy(muall, mu_out, loc.at[0, 0])]
    for k in range(steps):
        local.append(pltpu.make_async_copy(zs[k], zall_out.at[k, q], loc.at[k + 1, 0]))
        for e in peers:
            local.append(
                pltpu.make_async_copy(zfar.at[k, e - 1], zall_out.at[k, q ^ e], loc.at[k + 1, e])
            )
    for copy in local:
        copy.start()
    for copy in pending:
        copy.wait_send()
    for copy in local:
        copy.wait()


def sums_kernel(dcol, ccol, zall, mu, weighted, drift_out, control_out):
    i = pl.program_id(0)
    width = zall.shape[-1]

    def picked(c):
        return zall[:, :, c].astype(F32).reshape(-1, width).astype(BF16)

    drift_out[0] = jnp.dot(mu[0], picked(dcol[i]), preferred_element_type=F32)
    span = control_out.shape[2]
    for j in range(control_out.shape[0]):
        control_out[j, 0] = jnp.dot(
            weighted[0, j * span : (j + 1) * span, :], picked(ccol[j, i]),
            preferred_element_type=F32,
        )


def shards(
    drift_blocks, drift_cols, control_blocks, control_cols, controls, shooting_states, targets
):
    group_count, row_count = lax.axis_size("tm"), lax.axis_size("rows")
    rows, slots, width, _ = drift_blocks.shape
    nu = control_blocks.shape[0]
    if not (group_count == 2 * slots and slots == 4 and nu == 4 and row_count == 4 and targets.shape[0] == 5):
        return general(
            drift_blocks, drift_cols, control_blocks, control_cols, controls, shooting_states,
            targets,
        )
    steps, scen, local = targets.shape
    blocks = rows * row_count
    pairs = group_count // 2
    group_index = lax.axis_index("tm")
    pair, half = group_index // 2, group_index % 2
    first = jnp.swapaxes(shooting_states[0].reshape(scen, rows, width), 0, 1)
    nxt = passed_along(first, "tm", -1)
    tgt = jnp.swapaxes(targets.reshape(steps, scen, rows, width), 1, 2)
    wts = jnp.broadcast_to(
        jnp.swapaxes(controls, 0, 1)[..., None], (steps, nu, scen, width)
    )
    owner = jnp.concatenate([drift_cols.reshape(-1), control_cols.T.reshape(-1)])
    hits = (jnp.arange(blocks)[:, None] == owner[None]).astype(BF16)
    count = rows * (slots + nu)
    vmem = pl.BlockSpec(memory_space=pltpu.VMEM)
    smem = pl.BlockSpec(memory_space=pltpu.SMEM)
    hbm = pl.BlockSpec(memory_space=pl.ANY)
    dma = pltpu.SemaphoreType.DMA
    zshape = (steps, pairs, blocks, scen, width)
    mshape = (steps, pairs, rows, scen, width)
    zall, muall, lam, last, ig = pl.pallas_call(
        sweep_kernel,
        out_shape=(
            jax.ShapeDtypeStruct(zshape, BF16),
            jax.ShapeDtypeStruct(mshape, BF16),
            jax.ShapeDtypeStruct((rows, scen, width), F32),
            jax.ShapeDtypeStruct((rows, scen, width), BF16),
            jax.ShapeDtypeStruct((steps, nu, scen, width), F32),
        ),
        in_specs=[smem, smem] + [vmem] * 7,
        out_specs=(hbm, hbm, vmem, vmem, vmem),
        scratch_shapes=[
            *[pltpu.VMEM((blocks, scen, width), BF16) for _ in range(5)],
            pltpu.VMEM((steps, pairs - 1, blocks, scen, width), BF16),
            pltpu.VMEM(mshape, BF16),
            pltpu.VMEM((steps, nu, rows, scen, width), F32),
            pltpu.VMEM((scen * count, width), F32),
            pltpu.VMEM((blocks * scen, width), F32),
            pltpu.VMEM((steps, 3, rows, scen, width), BF16),
            pltpu.VMEM((steps, 3, rows, scen, width), BF16),
            dma((steps, 3)), dma((steps, 3)),
            dma((steps, 3, 2)), dma((steps, 3, 2)),
            dma((steps, 3, 2)), dma((steps, 3, 2)),
            dma((steps, 3)), dma((steps, 3)),
            dma((steps, 3)), dma((steps, 3)),
            dma((steps + 1, 4)),
        ],
        compiler_params=pltpu.CompilerParams(
            collective_id=0, has_side_effects=True, vmem_limit_bytes=60 * 2**20
        ),
        name="sweep",
    )(drift_cols, control_cols, drift_blocks, control_blocks, wts, first, nxt, tgt, hits)

    prev_end = passed_along(last, "tm", 1)
    prev_defect = jnp.where(group_index > 0, first.astype(F32) - prev_end.astype(F32), 0.0)
    grad_shooting = jnp.swapaxes(lam + defect_weight * prev_defect, 0, 1).reshape(1, scen, local)
    input_grads = jnp.swapaxes(jnp.sum(ig, -1), 0, 1)
    grad_controls = lax.psum(input_grads, "rows") * (local * row_count) ** (-0.5)
    grad_scale = (scen * steps * group_count) ** (-0.5)

    groups = [[i for i in range(group_count) if i % 2 == b] for b in range(2)]
    inputs = lax.all_gather(controls, "tm", axis_index_groups=groups)
    span = width // slots
    depth = steps * pairs * scen
    cut = lax.dynamic_slice_in_dim(muall, pair * span, span, 4).astype(F32)
    inputs = inputs.transpose(2, 0, 3, 1)[:, :, None, :, :, None]
    weighted = (cut[:, :, :, :, None, :] * inputs).astype(BF16)
    weighted = weighted.transpose(2, 4, 5, 0, 1, 3).reshape(rows, width, depth)
    mu_t = muall.transpose(2, 4, 0, 1, 3).reshape(rows, width, depth)
    dcol = lax.dynamic_index_in_dim(drift_cols, pair, 1, keepdims=False)
    drift_sum, control_sum = pl.pallas_call(
        sums_kernel,
        out_shape=(
            jax.ShapeDtypeStruct((rows, width, width), F32),
            jax.ShapeDtypeStruct((nu, rows, span, width), F32),
        ),
        grid_spec=pltpu.PrefetchScalarGridSpec(
            num_scalar_prefetch=2,
            grid=(rows,),
            in_specs=[
                pl.BlockSpec(zshape, lambda i, *_: (0, 0, 0, 0, 0), pipeline_mode=pl.Buffered(1)),
                pl.BlockSpec((1, width, depth), lambda i, *_: (i, 0, 0)),
                pl.BlockSpec((1, width, depth), lambda i, *_: (i, 0, 0)),
            ],
            out_specs=[
                pl.BlockSpec((1, width, width), lambda i, *_: (i, 0, 0)),
                pl.BlockSpec((nu, 1, span, width), lambda i, *_: (0, i, 0, 0)),
            ],
        ),
        name="sums",
    )(dcol, control_cols, zall, mu_t, weighted)
    drift_two = drift_sum.reshape(rows, 2, -1)
    control_two = control_sum.reshape(nu, rows, 2, -1)
    swap = [(i, i ^ 1) for i in range(group_count)]

    def merged(two, axis):
        mine = lax.dynamic_index_in_dim(two, half, axis, keepdims=False)
        other = lax.dynamic_index_in_dim(two, 1 - half, axis, keepdims=False)
        got = lax.ppermute(other.astype(BF16), "tm", swap)
        return (mine + got.astype(F32)) * grad_scale

    return (grad_shooting, grad_controls, merged(drift_two, 1), merged(control_two, 2))


def solution(mesh):
    return jax.shard_map(
        shards,
        mesh=mesh,
        in_specs=(
            P("rows", None, None, None),
            P("rows", None),
            P(None, "rows", None, None),
            P(None, "rows"),
            P(None, "tm", None),
            P("tm", None, "rows"),
            P("tm", None, "rows"),
        ),
        out_specs=(
            P("tm", None, "rows"),
            P(None, "tm", None),
            P("rows", "tm"),
            P(None, "rows", "tm"),
        ),
        check_vma=False,
    )
```

```python
import jax
import jax.numpy as jnp
from jax import lax
from jax.experimental import pallas as pl
from jax.experimental.pallas import tpu as pltpu
from jax.sharding import PartitionSpec as P

defect_weight = 2.0


def passed_along(value, axis, by):
    count = lax.axis_size(axis)
    pairs = [(i, i + by) for i in range(count) if 0 <= i + by < count]
    return lax.ppermute(value, axis, pairs)


def step_terms(gathered, block_width, drift_blocks, drift_cols, control_blocks, control_cols):
    blocks = gathered.reshape(gathered.shape[0], -1, block_width)
    picked = blocks[:, drift_cols]
    drift_out = jnp.einsum(
        "snki,nkoi->sno", picked, drift_blocks, preferred_element_type=jnp.float32
    )
    control_picked = blocks[:, control_cols]
    control_out = jnp.einsum(
        "sjni,jnoi->sjno", control_picked, control_blocks, preferred_element_type=jnp.float32
    )
    return (picked, drift_out, control_picked, control_out)


def general(
    drift_blocks, drift_cols, control_blocks, control_cols, controls, shooting_states, targets
):
    block_width = drift_blocks.shape[-1]
    scenarios = shooting_states.shape[1]
    local_rows = shooting_states.shape[2]
    horizon_steps = targets.shape[0]
    group_count = lax.axis_size("tm")
    group_index = lax.axis_index("tm")
    total_blocks = drift_blocks.shape[0] * lax.axis_size("rows")
    lifted_total = local_rows * lax.axis_size("rows")
    operators = (drift_blocks, drift_cols, control_blocks, control_cols)
    row_count = lax.axis_size("rows")
    targets_of = jnp.concatenate([drift_cols.reshape(-1), control_cols.reshape(-1)])
    hits = (targets_of[:, None] == jnp.arange(total_blocks)[None]).astype(jnp.bfloat16)
    first_panel = shooting_states[0]
    panels = [first_panel]
    stored = []
    state_panel = first_panel
    for position in range(horizon_steps):
        gathered = lax.all_gather(state_panel, "rows", axis=1, tiled=True)
        step_parts = step_terms(gathered, block_width, *operators)
        stored.append(step_parts)
        weights = controls[:, position].T[:, :, None, None]
        mixed = step_parts[1] + jnp.sum(weights * step_parts[3], axis=1)
        state_panel = mixed.reshape(scenarios, local_rows).astype(jnp.bfloat16)
        panels.append(state_panel)
    group_end = panels[-1]
    next_start = passed_along(first_panel, "tm", -1)
    prev_end = passed_along(group_end, "tm", 1)
    end_wide = group_end.astype(jnp.float32)
    defect = jnp.where(
        group_index < group_count - 1, next_start.astype(jnp.float32) - end_wide, 0.0
    )
    prev_defect = jnp.where(
        group_index > 0, first_panel.astype(jnp.float32) - prev_end.astype(jnp.float32), 0.0
    )
    adjoint = end_wide - targets[horizon_steps - 1].astype(jnp.float32) - defect_weight * defect
    input_grads = [None] * horizon_steps
    mu_list = []
    picked_list = []
    weighted_list = []
    control_picked_list = []
    for position in reversed(range(horizon_steps)):
        adjoint_half = adjoint.astype(jnp.bfloat16)
        picked, drift_out, control_picked, control_out = stored[position]
        mu_blocks = adjoint_half.reshape(scenarios, -1, block_width)
        mu_wide = mu_blocks.astype(jnp.float32)
        weights = controls[:, position].T[:, :, None, None]
        input_grads[position] = jnp.sum(mu_wide[:, None] * control_out, axis=(2, 3)).T
        weighted = (mu_wide[:, None] * weights).astype(jnp.bfloat16)
        mu_list.append(mu_blocks)
        picked_list.append(picked)
        weighted_list.append(weighted)
        control_picked_list.append(control_picked)
        drift_back = jnp.einsum(
            "sno,nkoi->snki", mu_blocks, drift_blocks, preferred_element_type=jnp.float32
        )
        control_back = (
            jnp.einsum(
                "sno,jnoi->sjni", mu_blocks, control_blocks, preferred_element_type=jnp.float32
            )
            * weights
        )
        terms = jnp.concatenate(
            [
                drift_back.reshape(scenarios, -1, block_width),
                control_back.reshape(scenarios, -1, block_width),
            ],
            1,
        ).astype(jnp.bfloat16)
        spread = jnp.einsum("gc,sgi->csi", hits, terms, preferred_element_type=jnp.float32)
        spread = spread.astype(jnp.bfloat16).reshape(row_count, -1, scenarios, block_width)
        shares = lax.all_to_all(spread, "rows", 0, 0)
        total = jnp.sum(shares.astype(jnp.float32), 0)
        adjoint = jnp.swapaxes(total, 0, 1).reshape(scenarios, local_rows)
        if position > 0:
            adjoint = (
                adjoint
                + panels[position].astype(jnp.float32)
                - targets[position - 1].astype(jnp.float32)
            )
    grad_shooting = (adjoint + defect_weight * prev_defect)[None]
    grad_controls = lax.psum(jnp.stack(input_grads, 1), "rows") * lifted_total ** (-0.5)
    grad_scale = (scenarios * horizon_steps * group_count) ** (-0.5)
    all_mu = jnp.concatenate(mu_list, 0)
    all_picked = jnp.concatenate(picked_list, 0)
    drift_sum = jnp.einsum("sno,snki->nkoi", all_mu, all_picked, preferred_element_type=jnp.float32)
    all_weighted = jnp.concatenate(weighted_list, 0)
    all_control_picked = jnp.concatenate(control_picked_list, 0)
    control_sum = jnp.einsum(
        "sjno,sjni->jnoi", all_weighted, all_control_picked, preferred_element_type=jnp.float32
    )
    drift_flat = drift_sum.reshape(drift_sum.shape[0], -1)
    grad_drift = lax.psum_scatter(drift_flat, "tm", scatter_dimension=1, tiled=True) * grad_scale
    control_flat = control_sum.reshape(control_sum.shape[0], control_sum.shape[1], -1)
    grad_control_ops = (
        lax.psum_scatter(control_flat, "tm", scatter_dimension=2, tiled=True) * grad_scale
    )
    return (grad_shooting, grad_controls, grad_drift, grad_control_ops)


MESH = pl.DeviceIdType.MESH
F32, BF16 = jnp.float32, jnp.bfloat16


def sweep_kernel(
    dcol, ccol, drift, control, wts, wex, start, tgt, hits,
    gshoot, ig, gdrift, gcontrol,
    z0, z1, z2, z3, z4, zfar, muall, bz, terms, spread, outbox, inbox,
    lam, last, nxt, before, igin, wfar, wall, cut, xd_out, xd_in, xc_out, xc_in,
    ag_s, ag_r, zl_s, zl_r, fw_s, fw_r, mu_s, mu_r, rs_s, rs_r,
    ig_s, ig_r, wx_s, wx_r, nb_s, nb_r, xd_s, xd_r, xc_s, xc_r,
):
    zs = (z0, z1, z2, z3, z4)
    steps, blocks, scen, width = muall.shape[0], *zfar.shape[2:]
    pairs = muall.shape[1]
    rows = start.shape[0]
    slots, nu = drift.shape[1], control.shape[0]
    count = rows * (slots + nu)
    tm, r = lax.axis_index("tm"), lax.axis_index("rows")
    q, x = tm // 2, tm % 2
    peers = range(1, 4)

    def row_peer(d):
        return {"tm": tm, "rows": r ^ d}

    def line_peer(e):
        return {"tm": 2 * (q ^ e) + x, "rows": r}

    barrier = pltpu.get_barrier_semaphore()
    for d in peers:
        pl.semaphore_signal(barrier, inc=1, device_id=row_peer(d), device_id_type=MESH)
        pl.semaphore_signal(barrier, inc=1, device_id=line_peer(d), device_id_type=MESH)
    group_count = lax.axis_size("tm")
    side = {"tm": tm ^ 1, "rows": r}
    after = {"tm": lax.rem(tm + 1, group_count), "rows": r}
    ahead = {"tm": lax.rem(tm + group_count - 1, group_count), "rows": r}
    for device in (side, after, ahead):
        pl.semaphore_signal(barrier, inc=1, device_id=device, device_id_type=MESH)
    pl.semaphore_wait(barrier, 9)
    pending = []

    def send(src, dst, s, t, to):
        copy = pltpu.make_async_remote_copy(
            src_ref=src, dst_ref=dst, send_sem=s, recv_sem=t, device_id=to, device_id_type=MESH
        )
        copy.start()
        pending.append(copy)
        return copy

    def panel(k, row):
        return zs[k].at[pl.ds(row * rows, rows)]

    def far(k, e, row):
        return zfar.at[k, e - 1, pl.ds(row * rows, rows)]

    def gather_start(k):
        return [
            send(panel(k, r), panel(k, r), ag_s.at[k, d - 1], ag_r.at[k, d - 1], row_peer(d))
            for d in peers
        ]

    def line_start(k):
        return [
            send(
                panel(k, r ^ (2 * h)), far(k, e, r ^ (2 * h)),
                zl_s.at[k, e - 1, h], zl_r.at[k, e - 1, h], line_peer(e),
            )
            for e in peers
            for h in range(2)
        ]

    def landed_line(k, e, h):
        there = far(k, e, r ^ (2 * h))
        return pltpu.make_async_remote_copy(
            src_ref=there, dst_ref=there, send_sem=zl_s.at[k, e - 1, h],
            recv_sem=zl_r.at[k, e - 1, h], device_id=line_peer(e), device_id_type=MESH,
        )

    def pass_on(k):
        for e in peers:
            for h in range(2):
                landed_line(k, e, h).wait_recv()
                there = far(k, e, r ^ (2 * h))
                send(there, there, fw_s.at[k, e - 1, h], fw_r.at[k, e - 1, h], row_peer(1))

    zs[0][pl.ds(r * rows, rows)] = start[...]
    first_step = gather_start(0)
    from_next = send(start, nxt, nb_s.at[0], nb_r.at[0], ahead)
    controls_in = [
        send(wex, wfar.at[e - 1], wx_s.at[e - 1], wx_r.at[e - 1], line_peer(e)) for e in peers
    ]
    for k in range(steps):
        for copy in first_step if k == 0 else gather_start(k):
            copy.wait_recv()
        line_start(k)

        def forward(i, carry):
            acc = jnp.zeros((scen, width), F32)
            for m in range(slots):
                acc += lax.dot_general(
                    zs[k][dcol[i, m]], drift[i, m], (((1,), (1,)), ((), ())),
                    preferred_element_type=F32,
                )
            for j in range(nu):
                part = lax.dot_general(
                    zs[k][ccol[j, i]], control[j, i], (((1,), (1,)), ((), ())),
                    preferred_element_type=F32,
                )
                bz[k, j, i] = part
                acc += wts[k, j] * part
            if k + 1 < steps:
                zs[k + 1][r * rows + i] = acc.astype(BF16)
            else:
                last[i] = acc.astype(BF16)
            return carry

        lax.fori_loop(0, rows, forward, 0, unroll=4)
    from_prev = send(last, before, nb_s.at[1], nb_r.at[1], after)
    from_next.wait_recv()
    ends = last[...].astype(F32)
    factor = jnp.where(tm < lax.axis_size("tm") - 1, defect_weight, 0.0)
    lam[...] = ends - tgt[steps - 1].astype(F32) - factor * (nxt[...].astype(F32) - ends)
    partial_in = []
    for k in reversed(range(steps)):
        muall[k, 0] = lam[...].astype(BF16)
        for e in peers:
            send(muall.at[k, 0], muall.at[k, e], mu_s.at[k, e - 1], mu_r.at[k, e - 1], line_peer(e))

        def backward(i, carry):
            mu = muall[k, 0, i]
            wide = mu.astype(F32)
            for m in range(slots):
                terms[pl.ds(i * slots + m, scen, stride=count), :] = jnp.dot(
                    mu, drift[i, m], preferred_element_type=F32
                )
            sums = []
            for j in range(nu):
                sums.append(carry[j] + wide * bz[k, j, i])
                terms[pl.ds(rows * slots + i * nu + j, scen, stride=count), :] = wts[k, j] * jnp.dot(
                    mu, control[j, i], preferred_element_type=F32
                )
            return tuple(sums)

        zero = jnp.zeros((scen, width), F32)
        sums = lax.fori_loop(0, rows, backward, (zero,) * nu, unroll=4)
        for j in range(nu):
            ig[k, j] = sums[j]
        for d in peers:
            partial_in.append(
                send(ig.at[k], igin.at[k, d - 1], ig_s.at[k, d - 1], ig_r.at[k, d - 1], row_peer(d))
            )
        for s in range(scen):
            spread[pl.ds(s, blocks, stride=scen), :] = jnp.dot(
                hits[...], terms[pl.ds(s * count, count), :].astype(BF16),
                preferred_element_type=F32,
            )

        def share(row):
            at = pl.multiple_of(row * (rows * scen), rows * scen)
            return spread[pl.ds(at, rows * scen), :].reshape(rows, scen, width)

        arriving = []
        for d in (2, 3, 1):
            outbox[k, d - 1] = share(r ^ d).astype(BF16)
            arriving.append(
                send(outbox.at[k, d - 1], inbox.at[k, d - 1], rs_s.at[k, d - 1], rs_r.at[k, d - 1], row_peer(d))
            )
        pass_on(steps - 1 - k)
        for copy in arriving:
            copy.wait_recv()
        total = share(r)
        for d in peers:
            total += inbox[k, d - 1].astype(F32)
        if k > 0:
            total += zs[k][pl.ds(r * rows, rows)].astype(F32) - tgt[k - 1].astype(F32)
        lam[...] = total
    for k in range(steps):
        for e in peers:
            theirs = muall.at[k, e]
            pltpu.make_async_remote_copy(
                src_ref=theirs, dst_ref=theirs, send_sem=mu_s.at[k, e - 1],
                recv_sem=mu_r.at[k, e - 1], device_id=line_peer(e), device_id_type=MESH,
            ).wait_recv()
            for h in range(2):
                there = far(k, e, r ^ 1 ^ (2 * h))
                pltpu.make_async_remote_copy(
                    src_ref=there, dst_ref=there, send_sem=fw_s.at[k, e - 1, h],
                    recv_sem=fw_r.at[k, e - 1, h], device_id=row_peer(1), device_id_type=MESH,
                ).wait_recv()
    from_prev.wait_recv()
    back = jnp.where(tm > 0, defect_weight, 0.0)
    gshoot[...] = lam[...] + back * (start[...].astype(F32) - before[...].astype(F32))
    for copy in controls_in:
        copy.wait_recv()
    for k in range(steps):
        for e in range(pairs):
            at = (k * pairs + e) * scen
            wall[at : at + scen, :] = wex[k] if e == 0 else wfar[e - 1, k]
    span = width // slots
    rowid = lax.broadcasted_iota(jnp.int32, (width, width), 0)
    laneid = lax.broadcasted_iota(jnp.int32, (width, width), 1)
    pick = jnp.where(rowid - span * q == laneid % span, 1.0, 0.0).astype(BF16)
    scale = (scen * steps * group_count) ** (-0.5)
    depth = steps * pairs * scen

    def picked(c):
        parts = []
        for k in range(steps):
            parts.append(zs[k][c].astype(F32))
            for e in range(pairs - 1):
                parts.append(zfar[k, e, c].astype(F32))
        return jnp.concatenate(parts, 0).astype(BF16)

    def sums_of(i, carry):
        mu = muall[:, :, i].astype(F32).reshape(depth, width)
        low = mu.astype(BF16)
        weighted = jnp.dot(low, pick, preferred_element_type=F32) * wall[...]
        mu_t = mu.T.astype(BF16)
        weighted_t = weighted.T.astype(BF16)
        cut[0] = jnp.dot(mu_t, picked(dcol[i, q]), preferred_element_type=F32) * scale
        gdrift[i] = cut[0, pl.ds(x * (width // 2), width // 2)]
        xd_out[i] = cut[0, pl.ds((1 - x) * (width // 2), width // 2)].astype(BF16)
        for j in range(nu):
            cut[1, :span] = (
                jnp.dot(
                    weighted_t[j * span : (j + 1) * span], picked(ccol[j, i]),
                    preferred_element_type=F32,
                )
                * scale
            )
            gcontrol[j, i] = cut[1, pl.ds(x * (span // 2), span // 2)]
            xc_out[i, j] = cut[1, pl.ds((1 - x) * (span // 2), span // 2)].astype(BF16)
        return carry

    crossing = []
    per = rows // xd_s.shape[0]
    for g in range(xd_s.shape[0]):
        lax.fori_loop(g * per, (g + 1) * per, sums_of, 0, unroll=2)
        part = pl.ds(g * per, per)
        crossing.append(
            (
                send(xd_out.at[part], xd_in.at[part], xd_s.at[g], xd_r.at[g], side),
                send(xc_out.at[part], xc_in.at[part], xc_s.at[g], xc_r.at[g], side),
            )
        )
    for copy in partial_in:
        copy.wait()
    ig[...] += igin[:, 0] + igin[:, 1] + igin[:, 2]
    for g, (one, two) in enumerate(crossing):
        one.wait_recv()
        two.wait_recv()
        part = pl.ds(g * per, per)
        gdrift[part] += xd_in[part].astype(F32)
        for j in range(nu):
            gcontrol[j, part] += xc_in[part, j].astype(F32)
    for copy in pending:
        if not any(copy is other for other in partial_in):
            copy.wait_send()


def shards(
    drift_blocks, drift_cols, control_blocks, control_cols, controls, shooting_states, targets
):
    group_count, row_count = lax.axis_size("tm"), lax.axis_size("rows")
    rows, slots, width, _ = drift_blocks.shape
    nu = control_blocks.shape[0]
    if not (group_count == 2 * slots and slots == 4 and nu == 4 and row_count == 4 and targets.shape[0] == 5):
        return general(
            drift_blocks, drift_cols, control_blocks, control_cols, controls, shooting_states,
            targets,
        )
    steps, scen, local = targets.shape
    blocks = rows * row_count
    pairs = group_count // 2
    first = jnp.swapaxes(shooting_states[0].reshape(scen, rows, width), 0, 1)
    tgt = jnp.swapaxes(targets.reshape(steps, scen, rows, width), 1, 2)
    wts = jnp.broadcast_to(
        jnp.swapaxes(controls, 0, 1)[..., None], (steps, nu, scen, width)
    )
    span = width // slots
    wex = jnp.repeat(controls.transpose(1, 2, 0), span, axis=2)
    owner = jnp.concatenate([drift_cols.reshape(-1), control_cols.T.reshape(-1)])
    hits = (jnp.arange(blocks)[:, None] == owner[None]).astype(BF16)
    count = rows * (slots + nu)
    vmem = pl.BlockSpec(memory_space=pltpu.VMEM)
    smem = pl.BlockSpec(memory_space=pltpu.SMEM)
    dma = pltpu.SemaphoreType.DMA
    groups = 8
    panel = (rows, scen, width)
    gshoot, ig, gdrift, gcontrol = pl.pallas_call(
        sweep_kernel,
        out_shape=(
            jax.ShapeDtypeStruct(panel, F32),
            jax.ShapeDtypeStruct((steps, nu, scen, width), F32),
            jax.ShapeDtypeStruct((rows, width // 2, width), F32),
            jax.ShapeDtypeStruct((nu, rows, span // 2, width), F32),
        ),
        in_specs=[smem, smem] + [vmem] * 7,
        out_specs=(vmem,) * 4,
        scratch_shapes=[
            *[pltpu.VMEM((blocks, scen, width), BF16) for _ in range(5)],
            pltpu.VMEM((steps, pairs - 1, blocks, scen, width), BF16),
            pltpu.VMEM((steps, pairs, rows, scen, width), BF16),
            pltpu.VMEM((steps, nu, rows, scen, width), F32),
            pltpu.VMEM((scen * count, width), F32),
            pltpu.VMEM((blocks * scen, width), F32),
            pltpu.VMEM((steps, 3, rows, scen, width), BF16),
            pltpu.VMEM((steps, 3, rows, scen, width), BF16),
            pltpu.VMEM(panel, F32),
            pltpu.VMEM(panel, BF16),
            pltpu.VMEM(panel, BF16),
            pltpu.VMEM(panel, BF16),
            pltpu.VMEM((steps, 3, nu, scen, width), F32),
            pltpu.VMEM((3, steps, scen, width), F32),
            pltpu.VMEM((steps * pairs * scen, width), F32),
            pltpu.VMEM((2, width, width), F32),
            pltpu.VMEM((rows, width // 2, width), BF16),
            pltpu.VMEM((rows, width // 2, width), BF16),
            pltpu.VMEM((rows, nu, span // 2, width), BF16),
            pltpu.VMEM((rows, nu, span // 2, width), BF16),
            dma((steps, 3)), dma((steps, 3)),
            dma((steps, 3, 2)), dma((steps, 3, 2)),
            dma((steps, 3, 2)), dma((steps, 3, 2)),
            dma((steps, 3)), dma((steps, 3)),
            dma((steps, 3)), dma((steps, 3)),
            dma((steps, 3)), dma((steps, 3)),
            dma((3,)), dma((3,)),
            dma((2,)), dma((2,)),
            dma((groups,)), dma((groups,)),
            dma((groups,)), dma((groups,)),
        ],
        compiler_params=pltpu.CompilerParams(
            collective_id=0, has_side_effects=True, vmem_limit_bytes=60 * 2**20
        ),
        name="sweep",
    )(drift_cols, control_cols, drift_blocks, control_blocks, wts, wex, first, tgt, hits)

    grad_shooting = jnp.swapaxes(gshoot, 0, 1).reshape(1, scen, local)
    input_grads = jnp.swapaxes(jnp.sum(ig, -1), 0, 1)
    grad_controls = input_grads * (local * row_count) ** (-0.5)
    return (
        grad_shooting,
        grad_controls,
        gdrift.reshape(rows, -1),
        gcontrol.reshape(nu, rows, -1),
    )


def solution(mesh):
    return jax.shard_map(
        shards,
        mesh=mesh,
        in_specs=(
            P("rows", None, None, None),
            P("rows", None),
            P(None, "rows", None, None),
            P(None, "rows"),
            P(None, "tm", None),
            P("tm", None, "rows"),
            P("tm", None, "rows"),
        ),
        out_specs=(
            P("tm", None, "rows"),
            P(None, "tm", None),
            P("rows", "tm"),
            P(None, "rows", "tm"),
        ),
        check_vma=False,
    )
```
